32 devices in a mesh: section: 2 (over core), row: 4 (over y, x), col: 4 (over z).
Axes of the slice: x: 2, y: 2, z: 4, core: 2. Of those that a mesh axis runs over, the one named last changes fastest.
Arguments:
- out_grad: bfloat16 [2048, 256], P(('row', 'col')), may hold values from -6 to 6
- pre_act: bfloat16 [2, 2048, 256], P('section', ('row', 'col')), may hold values from -6 to 6
- aggregated: bfloat16 [2, 2048, 256], P('section', ('row', 'col')), may hold values from -6 to 6
- weights: bfloat16 [2, 256, 256], P('section'), may hold values from -0.375 to 0.375
- tiles: bfloat16 [4, 4, 64, 128, 128], P('row', 'col'), may hold values from -0.109375 to 0.109375
- tile_index: int32 [4, 4, 64, 2], P('row', 'col'), may hold values from 0 to 3, as said below
- live_count: int32 [4, 4], P('row', 'col'), may hold values from 8 to 64, as said below
Outputs:
- weight_grad: float32 [2, 256, 256], P('section')
- feature_grads: bfloat16 [2, 2048, 256], P('section', ('row', 'col'))
The draws below stay inside these ranges and needn't reach their ends.
Inputs may be any that keep to these rules, and one draw needn't show every extreme that they name: `tile_index`: both entries index blocks of the tile: the first is under 4, the second under 4. `live_count`: some tile uses all 64 slots.
All inputs are finite; a program needn't handle non-finite values.
Results may differ from the reference program's by a relative error of at most 0.012.
Values may be sent and summed in bfloat16 or wider, within the bound.
A program may use at most 64 MiB of HBM per device.

```python
import math
import jax
import jax.numpy as jnp
from jax import lax

F = 256
BLOCK = 128
NODE_DEV = 128
SLOTS = 64
LAYERS = 2
NODES = 2048
TILE_ROWS = 512
ROW_BLOCKS = 4
COL_BLOCKS = 4
N_ROW = 4
N_COL = 4


def draw_tile_index(key, part):
    first, second = jax.random.split(jax.random.fold_in(key, 11))
    rows = jax.random.randint(first, (N_ROW, N_COL, SLOTS), 0, ROW_BLOCKS)
    cols = jax.random.randint(second, (N_ROW, N_COL, SLOTS), 0, COL_BLOCKS)
    rows = rows.at[0, 0, 0].set(ROW_BLOCKS - 1).at[0, 0, 1].set(0)
    cols = cols.at[0, 0, 0].set(COL_BLOCKS - 1).at[0, 0, 1].set(0)
    return jnp.stack([rows, cols], axis=-1).astype(jnp.int32)


def draw_live_count(key, part):
    first, second = jax.random.split(jax.random.fold_in(key, 23))
    lowest = max(1, SLOTS // 8)
    highest = max(lowest, SLOTS // 2)
    counts = jax.random.randint(first, (N_ROW * N_COL,), lowest, highest + 1)
    order = jax.random.permutation(second, N_ROW * N_COL)
    counts = counts.at[order[0]].set(SLOTS).at[order[1]].set(lowest)
    return counts.reshape(N_ROW, N_COL).astype(jnp.int32)


def steps_of(own_key, extent, cuts, low, top_value):
    factor_of = 1.0
    for position, shards_of in cuts:
        heights = jax.random.uniform(jax.random.fold_in(jax.random.fold_in(own_key, 6), position), (shards_of,), jnp.float32, low / len(cuts), top_value / len(cuts))
        factor_of = factor_of * jnp.repeat(jnp.exp(heights), extent[position] // shards_of).reshape((-1,) + (1,) * (len(extent) - 1 - position))
    return factor_of


def gaussian(own_key, shape, spread, bound, shards=(), kind=jnp.bfloat16):
    gain = steps_of(own_key, shape, shards, -0.22, 0.18) if shards else 1.0
    values = jax.random.normal(own_key, shape, jnp.float32) * spread * gain
    return jnp.minimum(jnp.maximum(values, -bound), bound).astype(kind)


def setup_inputs(seed: int = 0) -> dict:
    key_list = jax.random.split(jax.random.key(seed), 8)
    out_grad = gaussian(key_list[0], (NODES, F), 1.0, 6.0, ((0, 16),))
    pre_act = gaussian(key_list[1], (LAYERS, NODES, F), 1.0, 6.0, ((0, 2), (1, 16)))
    aggregated = gaussian(key_list[2], (LAYERS, NODES, F), 1.0, 6.0, ((0, 2), (1, 16)))
    weights = gaussian(key_list[3], (LAYERS, F, F), F ** -0.5, 0.375, ((0, 2),))
    tiles = gaussian(key_list[4], (N_ROW, N_COL, SLOTS, BLOCK, BLOCK), (16384 * SLOTS // (3 * NODE_DEV)) ** -0.5, 0.109375, ((0, 4), (1, 4)))
    tile_index = draw_tile_index(jax.random.fold_in(key_list[7], 71), 0)
    live_count = draw_live_count(jax.random.fold_in(key_list[7], 71), 0)
    return {"out_grad": out_grad, "pre_act": pre_act, "aggregated": aggregated, "weights": weights, "tiles": tiles, "tile_index": tile_index, "live_count": live_count}


def tile_apply(tile_blocks, tile_slots, tile_count, columns):
    width = columns.shape[1]
    col_blocks = columns.reshape(COL_BLOCKS, BLOCK, width)
    picked = jnp.take(col_blocks, tile_slots[:, 1], axis=0)
    products = jnp.einsum('sij,sjf->sif', tile_blocks.astype(jnp.float32), picked.astype(jnp.float32))
    slot_ids = jnp.arange(SLOTS, dtype=jnp.int32)
    live = slot_ids < tile_count
    targets = jnp.arange(ROW_BLOCKS, dtype=jnp.int32)
    select = ((tile_slots[:, 0][None, :] == targets[:, None]) & live[None, :]).astype(jnp.float32)
    summed = jnp.einsum('bs,sif->bif', select, products)
    return summed.reshape(TILE_ROWS, width)

def apply_graph(grad_rows, tiles, tile_index, live_count):
    pieces = grad_rows.reshape(N_ROW, N_COL, NODE_DEV, F)

    def one_row(row_id):

        def add_tile(total, col_id):
            columns = pieces[:, col_id].reshape(N_ROW * NODE_DEV, F)
            term = tile_apply(tiles[row_id, col_id], tile_index[row_id, col_id], live_count[row_id, col_id], columns)
            return (total + term, None)
        total, _ = lax.scan(add_tile, jnp.zeros((TILE_ROWS, F), jnp.float32), jnp.arange(N_COL, dtype=jnp.int32))
        return total
    stacked = lax.map(one_row, jnp.arange(N_ROW, dtype=jnp.int32))
    return stacked.reshape(NODES, F)

def layer_back(incoming, pre_layer, saved_agg, weight_mat, tiles, tile_index, live_count):
    masked = jnp.where(pre_layer > 0, incoming, jnp.zeros_like(incoming))
    weight_term = lax.dot_general(saved_agg, masked, (((0,), (0,)), ((), ())), preferred_element_type=jnp.float32)
    row_grad = lax.dot_general(masked, weight_mat, (((1,), (1,)), ((), ())), preferred_element_type=jnp.float32).astype(jnp.bfloat16)
    below = apply_graph(row_grad, tiles, tile_index, live_count).astype(jnp.bfloat16)
    return (weight_term, below)

def reference(out_grad, pre_act, aggregated, weights, tiles, tile_index, live_count):
    top_weight, hidden_grad = layer_back(out_grad, pre_act[1], aggregated[1], weights[1], tiles, tile_index, live_count)
    low_weight, input_grad = layer_back(hidden_grad, pre_act[0], aggregated[0], weights[0], tiles, tile_index, live_count)
    factor = 1.0 / math.sqrt(NODES)
    weight_grad = jnp.stack([low_weight, top_weight]) * factor
    feature_grads = jnp.stack([input_grad, hidden_grad])
    return (weight_grad, feature_grads)
```

```python
import functools
import math

import jax
import jax.numpy as jnp
from jax import lax
from jax.experimental import pallas as pl
from jax.experimental.pallas import tpu as pltpu
from jax.sharding import PartitionSpec as P

MESH = pl.DeviceIdType.MESH
CHUNKS = 4


def dense_kernel(col_blocks, slots, count, tiles, dense, held, total, sems):
    slot_total, block = held.shape[:2]
    per = slot_total // CHUNKS

    def fetch(part):
        rows = pl.ds(part * per, per)
        return pltpu.make_async_copy(tiles.at[rows], held.at[rows], sems.at[part])

    for part in range(CHUNKS):
        fetch(part).start()
    total[...] = jnp.zeros_like(total)
    live = count[0, 0]

    def add(slot, carry):
        place = slots[0, slot] * col_blocks + slots[1, slot]
        total[place] += held[slot].astype(jnp.float32)
        return carry

    for part in range(CHUNKS):
        fetch(part).wait()
        lax.fori_loop(part * per, jnp.minimum(live, (part + 1) * per), add, 0)
    for place in range(total.shape[0]):
        r, c = divmod(place, col_blocks)
        dense[pl.ds(r * block, block), pl.ds(c * block, block)] = total[place].astype(jnp.bfloat16)


def layers_kernel(
    R, C, scale, out_grad, pre, agg, weight, dense, wsum, feat,
    inc, gath, part, got, wire, wgot, wfull,
    row_send, row_recv, col_send, col_recv, ws_send, ws_recv, wg_send, wg_recv, hand_send, hand_recv,
):
    sec, r, c = (lax.axis_index(a) for a in ("section", "row", "col"))
    N = R * C
    me = r * C + c
    nodes, width = out_grad.shape
    chunk = wire.shape[1]

    def peer(p):
        return (sec, p // C, lax.rem(p, C))

    barrier = pltpu.get_barrier_semaphore()
    for d in range(1, N):
        pl.semaphore_signal(barrier, inc=1, device_id=peer(lax.rem(me + d, N)), device_id_type=MESH)
    pl.semaphore_signal(barrier, inc=1, device_id=(1 - sec, r, c), device_id_type=MESH)

    def copy(src, dst, send, recv, to):
        return pltpu.make_async_remote_copy(
            src_ref=src, dst_ref=dst, send_sem=send, recv_sem=recv, device_id=to, device_id_type=MESH
        )

    def row_copy(d, slot):
        return copy(gath.at[slot], gath.at[slot], row_send.at[d - 1], row_recv.at[d - 1], (sec, lax.rem(r + d, R), c))

    def col_copy(d, slot):
        to = lax.rem(c + d, C)
        return copy(part.at[d - 1], got.at[d - 1], col_send.at[d - 1], col_recv.at[d - 1], (sec, r, to))

    def ws_copy(d):
        to = lax.rem(me + d, N)
        return copy(wire.at[to], wgot.at[d - 1], ws_send.at[d - 1], ws_recv.at[d - 1], peer(to))

    def wg_copy(d, slot):
        return copy(wfull.at[slot], wfull.at[slot], wg_send.at[d - 1], wg_recv.at[d - 1], peer(lax.rem(me + d, N)))

    def hand_copy():
        return copy(feat, inc, hand_send, hand_recv, (1 - sec, r, c))

    @pl.when(sec == 1)
    def _():
        inc[...] = out_grad[...]

    pl.semaphore_wait(barrier, N)

    @pl.when(sec == 0)
    def _():
        hand_copy().wait_recv()

    masked = jnp.where(pre[...] > 0, inc[...], jnp.zeros((nodes, width), jnp.bfloat16))
    gath[r] = lax.dot_general(
        masked, weight[...], (((1,), (1,)), ((), ())), preferred_element_type=jnp.float32
    ).astype(jnp.bfloat16)
    for d in range(1, R):
        row_copy(d, r).start()

    wire[...] = lax.dot_general(
        agg[...], masked, (((0,), (0,)), ((), ())), preferred_element_type=jnp.float32
    ).astype(jnp.bfloat16).reshape(wire.shape)

    def start_weight():
        for d in range(1, N):
            ws_copy(d).start()

    def gather_weight():
        total = wire[me].astype(jnp.float32)
        for d in range(1, N):
            ws_copy(d).wait_recv()
            total = total + wgot[d - 1].astype(jnp.float32)
        wfull[me] = (total * scale).astype(jnp.bfloat16)
        for d in range(1, N):
            wg_copy(d, me).start()

    @pl.when(sec == 0)
    def _():
        start_weight()

    for d in range(1, R):
        row_copy(d, lax.rem(r + R - d, R)).wait_recv()
    spread = gath[...].reshape(R * nodes, width)

    def term(to):
        rows = pl.ds(pl.multiple_of(to * nodes, nodes), nodes)
        return jnp.dot(dense[rows, :], spread, preferred_element_type=jnp.float32)

    for d in range(1, C):
        part[d - 1] = term(lax.rem(c + d, C)).astype(jnp.bfloat16)
        col_copy(d, c).start()
    total = term(c)

    @pl.when(sec == 0)
    def _():
        gather_weight()

    for d in range(1, C):
        col_copy(d, c).wait_recv()
        total = total + got[d - 1].astype(jnp.float32)
    feat[...] = total.astype(jnp.bfloat16)

    @pl.when(sec == 1)
    def _():
        hand_copy().start()
        start_weight()
        gather_weight()
        hand_copy().wait_send()

    for d in range(1, N):
        wg_copy(d, lax.rem(me + N - d, N)).wait_recv()
    wsum[...] = wfull[...]
    for d in range(1, R):
        row_copy(d, r).wait_send()
    for d in range(1, C):
        col_copy(d, c).wait_send()
    for d in range(1, N):
        ws_copy(d).wait_send()
        wg_copy(d, me).wait_send()


def fused(out_grad, pre_act, aggregated, weights, tiles, tile_index, live_count):
    R, C = lax.axis_size("row"), lax.axis_size("col")
    N = R * C
    nodes, width = out_grad.shape
    slot_total, block = tiles.shape[2:4]
    rows, cols = C * nodes, R * nodes
    row_blocks, col_blocks = rows // block, cols // block
    vmem = pl.BlockSpec(memory_space=pltpu.VMEM)
    smem = pl.BlockSpec(memory_space=pltpu.SMEM)
    bf16, f32, dma = jnp.bfloat16, jnp.float32, pltpu.SemaphoreType.DMA
    dense = pl.pallas_call(
        functools.partial(dense_kernel, col_blocks),
        out_shape=jax.ShapeDtypeStruct((rows, cols), bf16),
        in_specs=[smem, smem, pl.BlockSpec(memory_space=pl.ANY)],
        out_specs=vmem,
        scratch_shapes=[
            pltpu.VMEM((slot_total, block, block), bf16),
            pltpu.VMEM((row_blocks * col_blocks, block, block), f32),
            dma((CHUNKS,)),
        ],
        name="dense_tile",
    )(tile_index[0, 0].T, live_count, tiles[0, 0])
    chunk = width // N
    scale = 1.0 / math.sqrt(nodes * N)
    wsum, feat = pl.pallas_call(
        functools.partial(layers_kernel, R, C, scale),
        out_shape=(
            jax.ShapeDtypeStruct((N, chunk, width), bf16),
            jax.ShapeDtypeStruct((nodes, width), bf16),
        ),
        in_specs=[vmem] * 5,
        out_specs=(vmem, vmem),
        scratch_shapes=[
            pltpu.VMEM((nodes, width), bf16),
            pltpu.VMEM((R, nodes, width), bf16),
            pltpu.VMEM((C - 1, nodes, width), bf16),
            pltpu.VMEM((C - 1, nodes, width), bf16),
            pltpu.VMEM((N, chunk, width), bf16),
            pltpu.VMEM((N - 1, chunk, width), bf16),
            pltpu.VMEM((N, chunk, width), bf16),
            dma((R - 1,)), dma((R - 1,)), dma((C - 1,)), dma((C - 1,)),
            dma((N - 1,)), dma((N - 1,)), dma((N - 1,)), dma((N - 1,)), dma, dma,
        ],
        compiler_params=pltpu.CompilerParams(collective_id=0, has_side_effects=True),
        name="both_layers",
    )(out_grad, pre_act[0], aggregated[0], weights[0], dense)
    return (wsum.astype(f32).reshape(1, width, width), feat[None])


def from_behind(value, axis, steps):
    count = lax.axis_size(axis)
    leading, last = (max(0, -steps), min(count, count - steps))
    return lax.ppermute(value, axis, [(source, source + steps) for source in range(leading, last)])


def on_device(out_grad, pre_act, aggregated, weights, tiles, tile_index, live_count):
    nodes, width = out_grad.shape
    devices = lax.axis_size("row") * lax.axis_size("col")
    dense_blocks = devices * (nodes // tiles.shape[3]) ** 2
    if dense_blocks <= tiles.shape[2] and width % (16 * devices) == 0:
        return fused(out_grad, pre_act, aggregated, weights, tiles, tile_index, live_count)
    section_id = lax.axis_index("section")
    upper = section_id == 1
    pre_layer = pre_act[0]
    saved_agg = aggregated[0]
    weight_mat = weights[0]
    tile_blocks = tiles[0, 0]
    tile_slots = tile_index[0, 0]
    tile_count = live_count[0, 0]
    node_rows = out_grad.shape[0]
    width = out_grad.shape[1]
    slot_total = tile_blocks.shape[0]
    block = tile_blocks.shape[1]
    tile_rows = node_rows * lax.axis_size("col")
    row_blocks = tile_rows // block
    group = min(32, slot_total)
    groups = slot_total // group
    grouped_slots = tile_slots.reshape(groups, group, 2)
    all_targets = jnp.arange(row_blocks, dtype=jnp.int32)

    def spread(row_grad):
        return lax.all_gather(row_grad, "row", axis=0, tiled=True)

    def block_total(source, col_blocks):
        height = source.shape[1]
        grouped_blocks = source.reshape(groups, group, height, block)

        def group_term(total, blocks_here, slots_here, first_slot):
            picked = jnp.take(col_blocks, slots_here[:, 1], axis=0)
            products = jnp.einsum(
                "sij,sjf->sif", blocks_here, picked, preferred_element_type=jnp.float32
            )
            slot_ids = first_slot + jnp.arange(group, dtype=jnp.int32)
            live = slot_ids < tile_count
            select = ((slots_here[:, 0][None, :] == all_targets[:, None]) & live[None, :]).astype(
                jnp.float32
            )
            return total + jnp.einsum("bs,sif->bif", select, products)

        start_total = jnp.zeros((row_blocks, height, width), jnp.float32)

        def scan_step(total, group_id):
            blocks_here = lax.dynamic_index_in_dim(grouped_blocks, group_id, 0, False)
            slots_here = lax.dynamic_index_in_dim(grouped_slots, group_id, 0, False)
            return (group_term(total, blocks_here, slots_here, group_id * group), None)

        total, _ = lax.scan(scan_step, start_total, jnp.arange(groups, dtype=jnp.int32))
        return total.reshape(row_blocks * height, width)

    def reduce_col(source, gathered):
        col_blocks = gathered.reshape(-1, block, width)
        height = source.shape[1]
        return lax.psum_scatter(
            block_total(source, col_blocks), "col", scatter_dimension=0, tiled=True
        )

    def local_terms(incoming):
        masked = jnp.where(pre_layer > 0, incoming, jnp.zeros_like(incoming))
        weight_term = lax.dot_general(
            saved_agg, masked, (((0,), (0,)), ((), ())), preferred_element_type=jnp.float32
        )
        row_grad = lax.dot_general(
            masked, weight_mat, (((1,), (1,)), ((), ())), preferred_element_type=jnp.float32
        ).astype(jnp.bfloat16)
        return (weight_term, row_grad)

    def backward_step(incoming):
        weight_term, row_grad = local_terms(incoming)
        summed = reduce_col(tile_blocks, spread(row_grad))
        return (weight_term, summed.astype(jnp.bfloat16))

    first_input = jnp.where(upper, out_grad, jnp.zeros_like(out_grad))
    first_weight, first_grad = backward_step(first_input)
    received = from_behind(first_grad, "section", -1)
    second_weight, second_grad = backward_step(received)
    local_weight = jnp.where(upper, first_weight, second_weight)
    feature_block = jnp.where(upper, first_grad, second_grad)
    total_weight = lax.psum(local_weight, ("row", "col"))
    node_total = node_rows * lax.axis_size("row") * lax.axis_size("col")
    weight_grad = (total_weight * (1.0 / math.sqrt(node_total)))[None]
    return (weight_grad, feature_block[None])


def solution(mesh):
    placed = (
        P(("row", "col"), None),
        P("section", ("row", "col"), None),
        P("section", ("row", "col"), None),
        P("section", None, None),
        P("row", "col", None, None, None),
        P("row", "col", None, None),
        P("row", "col"),
    )
    return jax.shard_map(
        on_device,
        mesh=mesh,
        in_specs=placed,
        out_specs=(P("section", None, None), P("section", ("row", "col"), None)),
        check_vma=False,
    )
```

```python
import functools
import math

import jax
import jax.numpy as jnp
from jax import lax
from jax.experimental import pallas as pl
from jax.experimental.pallas import tpu as pltpu
from jax.sharding import PartitionSpec as P

MESH = pl.DeviceIdType.MESH
CHUNKS = 4


def dense_kernel(col_blocks, slots, count, tiles, dense, held, total, sems):
    slot_total, block = held.shape[:2]
    per = slot_total // CHUNKS

    def fetch(part):
        rows = pl.ds(part * per, per)
        return pltpu.make_async_copy(tiles.at[rows], held.at[rows], sems.at[part])

    for part in range(CHUNKS):
        fetch(part).start()
    total[...] = jnp.zeros_like(total)
    live = count[0, 0]

    def add(slot, carry):
        place = slots[0, slot] * col_blocks + slots[1, slot]
        total[place] += held[slot].astype(jnp.float32)
        return carry

    for part in range(CHUNKS):
        fetch(part).wait()
        lax.fori_loop(part * per, jnp.minimum(live, (part + 1) * per), add, 0)
    for place in range(total.shape[0]):
        r, c = divmod(place, col_blocks)
        dense[pl.ds(r * block, block), pl.ds(c * block, block)] = total[place].astype(jnp.bfloat16)


def layers_kernel(
    R, C, scale, out_grad, pre, agg, weight, dense, wsum, feat,
    inc, gath, part, got, wire, xgot, along, summed,
    row_send, row_recv, col_send, col_recv, hand_send, hand_recv,
    wx_send, wx_recv, wz_send, wz_recv, wg_send, wg_recv,
):
    sec, r, c = (lax.axis_index(a) for a in ("section", "row", "col"))
    nodes, width = out_grad.shape

    def row_peer(d):
        return (sec, lax.rem(r + d, R), c)

    def col_peer(d):
        return (sec, r, lax.rem(c + d, C))

    across = (1 - sec, r, c)
    barrier = pltpu.get_barrier_semaphore()
    peers = [row_peer(d) for d in range(1, R)] + [col_peer(d) for d in range(1, C)] + [across]
    for to in peers:
        pl.semaphore_signal(barrier, inc=1, device_id=to, device_id_type=MESH)

    def copy(src, dst, send, recv, to):
        return pltpu.make_async_remote_copy(
            src_ref=src, dst_ref=dst, send_sem=send, recv_sem=recv, device_id=to, device_id_type=MESH
        )

    def row_copy(d, slot):
        return copy(gath.at[slot], gath.at[slot], row_send.at[d - 1], row_recv.at[d - 1], row_peer(d))

    def col_copy(d):
        return copy(part.at[d - 1], got.at[d - 1], col_send.at[d - 1], col_recv.at[d - 1], col_peer(d))

    def hand_copy():
        return copy(feat, inc, hand_send, hand_recv, across)

    def wx_copy(d):
        to = lax.rem(r + d, R)
        return copy(wire.at[to], xgot.at[d - 1], wx_send.at[d - 1], wx_recv.at[d - 1], row_peer(d))

    def wz_copy(d, slot):
        return copy(along.at[slot], along.at[slot], wz_send.at[d - 1], wz_recv.at[d - 1], col_peer(d))

    def wg_copy(d, slot):
        return copy(summed.at[slot], summed.at[slot], wg_send.at[d - 1], wg_recv.at[d - 1], row_peer(d))

    def own_rows():
        masked = jnp.where(pre[...] > 0, inc[...], jnp.zeros((nodes, width), jnp.bfloat16))
        inc[...] = masked
        gath[r] = lax.dot_general(
            masked, weight[...], (((1,), (1,)), ((), ())), preferred_element_type=jnp.float32
        ).astype(jnp.bfloat16)

    @pl.when(sec == 1)
    def _():
        inc[...] = out_grad[...]
        own_rows()

    pl.semaphore_wait(barrier, len(peers))

    @pl.when(sec == 0)
    def _():
        hand_copy().wait_recv()
        own_rows()

    for d in range(1, R):
        row_copy(d, r).start()

    wire[...] = lax.dot_general(
        agg[...], inc[...], (((0,), (0,)), ((), ())), preferred_element_type=jnp.float32
    ).astype(jnp.bfloat16).reshape(wire.shape)
    for d in range(1, R):
        wx_copy(d).start()

    for d in range(1, R):
        row_copy(d, lax.rem(r + R - d, R)).wait_recv()
    spread = gath[...].reshape(R * nodes, width)

    def term(to):
        rows = pl.ds(pl.multiple_of(to * nodes, nodes), nodes)
        return jnp.dot(dense[rows, :], spread, preferred_element_type=jnp.float32)

    for d in range(1, C):
        part[d - 1] = term(lax.rem(c + d, C)).astype(jnp.bfloat16)
        col_copy(d).start()
    total = term(c)

    def weight_along():
        here = wire[r].astype(jnp.float32)
        for d in range(1, R):
            wx_copy(d).wait_recv()
            here = here + xgot[d - 1].astype(jnp.float32)
        along[c] = here.astype(jnp.bfloat16)
        for d in range(1, C):
            wz_copy(d, c).start()

    @pl.when(sec == 0)
    def _():
        weight_along()

    for d in range(1, C):
        col_copy(d).wait_recv()
        total = total + got[d - 1].astype(jnp.float32)
    feat[...] = total.astype(jnp.bfloat16)

    @pl.when(sec == 1)
    def _():
        hand_copy().start()
        weight_along()
        hand_copy().wait_send()

    for d in range(1, C):
        wz_copy(d, lax.rem(c + C - d, C)).wait_recv()
    whole = along[0].astype(jnp.float32)
    for k in range(1, C):
        whole = whole + along[k].astype(jnp.float32)
    summed[r] = (whole * scale).astype(jnp.bfloat16)
    for d in range(1, R):
        wg_copy(d, r).start()
    for d in range(1, R):
        wg_copy(d, lax.rem(r + R - d, R)).wait_recv()
    wsum[...] = summed[...].reshape(wsum.shape)
    for d in range(1, R):
        row_copy(d, r).wait_send()
        wx_copy(d).wait_send()
        wg_copy(d, r).wait_send()
    for d in range(1, C):
        col_copy(d).wait_send()
        wz_copy(d, c).wait_send()


def finish_kernel(wsum, feat, weight_grad, feature_grads):
    weight_grad[...] = wsum[...].astype(jnp.float32)
    feature_grads[...] = feat[...]


def fused(out_grad, pre_act, aggregated, weights, tiles, tile_index, live_count):
    R, C = lax.axis_size("row"), lax.axis_size("col")
    N = R * C
    nodes, width = out_grad.shape
    slot_total, block = tiles.shape[2:4]
    rows, cols = C * nodes, R * nodes
    row_blocks, col_blocks = rows // block, cols // block
    vmem = pl.BlockSpec(memory_space=pltpu.VMEM)
    smem = pl.BlockSpec(memory_space=pltpu.SMEM)
    bf16, f32, dma = jnp.bfloat16, jnp.float32, pltpu.SemaphoreType.DMA
    dense = pl.pallas_call(
        functools.partial(dense_kernel, col_blocks),
        out_shape=jax.ShapeDtypeStruct((rows, cols), bf16),
        in_specs=[smem, smem, pl.BlockSpec(memory_space=pl.ANY)],
        out_specs=vmem,
        scratch_shapes=[
            pltpu.VMEM((slot_total, block, block), bf16),
            pltpu.VMEM((row_blocks * col_blocks, block, block), f32),
            dma((CHUNKS,)),
        ],
        name="dense_tile",
    )(tile_index[0, 0].T, live_count, tiles[0, 0])
    share = width // R
    scale = 1.0 / math.sqrt(nodes * N)
    wsum, feat = pl.pallas_call(
        functools.partial(layers_kernel, R, C, scale),
        out_shape=(
            jax.ShapeDtypeStruct((width, width), bf16),
            jax.ShapeDtypeStruct((nodes, width), bf16),
        ),
        in_specs=[vmem] * 5,
        out_specs=(vmem, vmem),
        scratch_shapes=[
            pltpu.VMEM((nodes, width), bf16),
            pltpu.VMEM((R, nodes, width), bf16),
            pltpu.VMEM((C - 1, nodes, width), bf16),
            pltpu.VMEM((C - 1, nodes, width), bf16),
            pltpu.VMEM((R, share, width), bf16),
            pltpu.VMEM((R - 1, share, width), bf16),
            pltpu.VMEM((C, share, width), bf16),
            pltpu.VMEM((R, share, width), bf16),
            dma((R - 1,)), dma((R - 1,)), dma((C - 1,)), dma((C - 1,)), dma, dma,
            dma((R - 1,)), dma((R - 1,)), dma((C - 1,)), dma((C - 1,)), dma((R - 1,)), dma((R - 1,)),
        ],
        compiler_params=pltpu.CompilerParams(collective_id=0, has_side_effects=True),
        name="both_layers",
    )(out_grad, pre_act[0], aggregated[0], weights[0], dense)
    weight_grad, feature_grads = pl.pallas_call(
        finish_kernel,
        out_shape=(
            jax.ShapeDtypeStruct((width, width), f32),
            jax.ShapeDtypeStruct((nodes, width), bf16),
        ),
        in_specs=[vmem] * 2,
        out_specs=(vmem, vmem),
        name="finish",
    )(wsum, feat)
    return (weight_grad[None], feature_grads[None])


def from_behind(value, axis, steps):
    count = lax.axis_size(axis)
    leading, last = (max(0, -steps), min(count, count - steps))
    return lax.ppermute(value, axis, [(source, source + steps) for source in range(leading, last)])


def on_device(out_grad, pre_act, aggregated, weights, tiles, tile_index, live_count):
    nodes, width = out_grad.shape
    devices = lax.axis_size("row") * lax.axis_size("col")
    dense_blocks = devices * (nodes // tiles.shape[3]) ** 2
    if dense_blocks <= tiles.shape[2] and width % (16 * devices) == 0:
        return fused(out_grad, pre_act, aggregated, weights, tiles, tile_index, live_count)
    section_id = lax.axis_index("section")
    upper = section_id == 1
    pre_layer = pre_act[0]
    saved_agg = aggregated[0]
    weight_mat = weights[0]
    tile_blocks = tiles[0, 0]
    tile_slots = tile_index[0, 0]
    tile_count = live_count[0, 0]
    node_rows = out_grad.shape[0]
    width = out_grad.shape[1]
    slot_total = tile_blocks.shape[0]
    block = tile_blocks.shape[1]
    tile_rows = node_rows * lax.axis_size("col")
    row_blocks = tile_rows // block
    group = min(32, slot_total)
    groups = slot_total // group
    grouped_slots = tile_slots.reshape(groups, group, 2)
    all_targets = jnp.arange(row_blocks, dtype=jnp.int32)

    def spread(row_grad):
        return lax.all_gather(row_grad, "row", axis=0, tiled=True)

    def block_total(source, col_blocks):
        height = source.shape[1]
        grouped_blocks = source.reshape(groups, group, height, block)

        def group_term(total, blocks_here, slots_here, first_slot):
            picked = jnp.take(col_blocks, slots_here[:, 1], axis=0)
            products = jnp.einsum(
                "sij,sjf->sif", blocks_here, picked, preferred_element_type=jnp.float32
            )
            slot_ids = first_slot + jnp.arange(group, dtype=jnp.int32)
            live = slot_ids < tile_count
            select = ((slots_here[:, 0][None, :] == all_targets[:, None]) & live[None, :]).astype(
                jnp.float32
            )
            return total + jnp.einsum("bs,sif->bif", select, products)

        start_total = jnp.zeros((row_blocks, height, width), jnp.float32)

        def scan_step(total, group_id):
            blocks_here = lax.dynamic_index_in_dim(grouped_blocks, group_id, 0, False)
            slots_here = lax.dynamic_index_in_dim(grouped_slots, group_id, 0, False)
            return (group_term(total, blocks_here, slots_here, group_id * group), None)

        total, _ = lax.scan(scan_step, start_total, jnp.arange(groups, dtype=jnp.int32))
        return total.reshape(row_blocks * height, width)

    def reduce_col(source, gathered):
        col_blocks = gathered.reshape(-1, block, width)
        height = source.shape[1]
        return lax.psum_scatter(
            block_total(source, col_blocks), "col", scatter_dimension=0, tiled=True
        )

    def local_terms(incoming):
        masked = jnp.where(pre_layer > 0, incoming, jnp.zeros_like(incoming))
        weight_term = lax.dot_general(
            saved_agg, masked, (((0,), (0,)), ((), ())), preferred_element_type=jnp.float32
        )
        row_grad = lax.dot_general(
            masked, weight_mat, (((1,), (1,)), ((), ())), preferred_element_type=jnp.float32
        ).astype(jnp.bfloat16)
        return (weight_term, row_grad)

    def backward_step(incoming):
        weight_term, row_grad = local_terms(incoming)
        summed = reduce_col(tile_blocks, spread(row_grad))
        return (weight_term, summed.astype(jnp.bfloat16))

    first_input = jnp.where(upper, out_grad, jnp.zeros_like(out_grad))
    first_weight, first_grad = backward_step(first_input)
    received = from_behind(first_grad, "section", -1)
    second_weight, second_grad = backward_step(received)
    local_weight = jnp.where(upper, first_weight, second_weight)
    feature_block = jnp.where(upper, first_grad, second_grad)
    total_weight = lax.psum(local_weight, ("row", "col"))
    node_total = node_rows * lax.axis_size("row") * lax.axis_size("col")
    weight_grad = (total_weight * (1.0 / math.sqrt(node_total)))[None]
    return (weight_grad, feature_block[None])


def solution(mesh):
    placed = (
        P(("row", "col"), None),
        P("section", ("row", "col"), None),
        P("section", ("row", "col"), None),
        P("section", None, None),
        P("row", "col", None, None, None),
        P("row", "col", None, None),
        P("row", "col"),
    )
    return jax.shard_map(
        on_device,
        mesh=mesh,
        in_specs=placed,
        out_specs=(P("section", None, None), P("section", ("row", "col"), None)),
        check_vma=False,
    )
```

```python
import functools
import math

import jax
import jax.numpy as jnp
from jax import lax
from jax.experimental import pallas as pl
from jax.experimental.pallas import tpu as pltpu
from jax.sharding import PartitionSpec as P

MESH = pl.DeviceIdType.MESH
CHUNKS = 4


def dense_kernel(col_blocks, slots, count, tiles, dense, held, total, sems):
    slot_total, block = held.shape[:2]
    per = slot_total // CHUNKS

    def fetch(part):
        rows = pl.ds(part * per, per)
        return pltpu.make_async_copy(tiles.at[rows], held.at[rows], sems.at[part])

    for part in range(CHUNKS):
        fetch(part).start()
    total[...] = jnp.zeros_like(total)
    live = count[0, 0]

    def add(slot, carry):
        place = slots[0, slot] * col_blocks + slots[1, slot]
        total[place] += held[slot].astype(jnp.float32)
        return carry

    for part in range(CHUNKS):
        fetch(part).wait()
        lax.fori_loop(part * per, jnp.minimum(live, (part + 1) * per), add, 0)
    for place in range(total.shape[0]):
        r, c = divmod(place, col_blocks)
        dense[pl.ds(r * block, block), pl.ds(c * block, block)] = total[place].astype(jnp.bfloat16)


def layers_kernel(
    R, C, scale, out_grad, pre_act, aggregated, weights, dense_tile, wsum, feat,
    pre, agg, weight, dense, in_sems, inc, gath, part, got, wire, xgot, along, summed,
    row_send, row_recv, col_send, col_recv, hand_send, hand_recv,
    wx_send, wx_recv, wz_send, wz_recv, wg_send, wg_recv,
):
    sec, r, c = (lax.axis_index(a) for a in ("section", "row", "col"))
    nodes, width = inc.shape

    def row_peer(d):
        return (sec, lax.rem(r + d, R), c)

    def col_peer(d):
        return (sec, r, lax.rem(c + d, C))

    across = (1 - sec, r, c)
    barrier = pltpu.get_barrier_semaphore()
    peers = [row_peer(d) for d in range(1, R)] + [col_peer(d) for d in range(1, C)] + [across]
    for to in peers:
        pl.semaphore_signal(barrier, inc=1, device_id=to, device_id_type=MESH)

    load_inc = pltpu.make_async_copy(out_grad, inc, in_sems.at[0])
    load_pre = pltpu.make_async_copy(pre_act, pre, in_sems.at[1])
    load_weight = pltpu.make_async_copy(weights, weight, in_sems.at[2])
    load_agg = pltpu.make_async_copy(aggregated, agg, in_sems.at[3])
    load_dense = pltpu.make_async_copy(dense_tile, dense, in_sems.at[4])

    @pl.when(sec == 1)
    def _():
        load_inc.start()

    load_pre.start()
    load_weight.start()
    load_agg.start()
    load_dense.start()

    def copy(src, dst, send, recv, to):
        return pltpu.make_async_remote_copy(
            src_ref=src, dst_ref=dst, send_sem=send, recv_sem=recv, device_id=to, device_id_type=MESH
        )

    def row_copy(d, slot):
        return copy(gath.at[slot], gath.at[slot], row_send.at[d - 1], row_recv.at[d - 1], row_peer(d))

    def col_copy(d):
        return copy(part.at[d - 1], got.at[d - 1], col_send.at[d - 1], col_recv.at[d - 1], col_peer(d))

    def hand_copy():
        return copy(feat, inc, hand_send, hand_recv, across)

    def wx_copy(d):
        to = lax.rem(r + d, R)
        return copy(wire.at[to], xgot.at[d - 1], wx_send.at[d - 1], wx_recv.at[d - 1], row_peer(d))

    def wz_copy(d, slot):
        return copy(along.at[slot], along.at[slot], wz_send.at[d - 1], wz_recv.at[d - 1], col_peer(d))

    def wg_copy(d, slot):
        return copy(summed.at[slot], summed.at[slot], wg_send.at[d - 1], wg_recv.at[d - 1], row_peer(d))

    def own_rows():
        masked = jnp.where(pre[...] > 0, inc[...], jnp.zeros((nodes, width), jnp.bfloat16))
        inc[...] = masked
        gath[r] = lax.dot_general(
            masked, weight[...], (((1,), (1,)), ((), ())), preferred_element_type=jnp.float32
        ).astype(jnp.bfloat16)

    load_pre.wait()
    load_weight.wait()

    @pl.when(sec == 1)
    def _():
        load_inc.wait()
        own_rows()

    pl.semaphore_wait(barrier, len(peers))

    @pl.when(sec == 0)
    def _():
        hand_copy().wait_recv()
        own_rows()

    for d in range(1, R):
        row_copy(d, r).start()

    load_agg.wait()
    wire[...] = lax.dot_general(
        agg[...], inc[...], (((0,), (0,)), ((), ())), preferred_element_type=jnp.float32
    ).astype(jnp.bfloat16).reshape(wire.shape)
    for d in range(1, R):
        wx_copy(d).start()

    for d in range(1, R):
        row_copy(d, lax.rem(r + R - d, R)).wait_recv()
    load_dense.wait()

    def weight_along():
        here = wire[r].astype(jnp.float32)
        for d in range(1, R):
            wx_copy(d).wait_recv()
            here = here + xgot[d - 1].astype(jnp.float32)
        along[c] = here.astype(jnp.bfloat16)
        for d in range(1, C):
            wz_copy(d, c).start()

    def weight_back():
        for d in range(1, C):
            wz_copy(d, lax.rem(c + C - d, C)).wait_recv()
        whole = along[0].astype(jnp.float32)
        for k in range(1, C):
            whole = whole + along[k].astype(jnp.float32)
        summed[r] = (whole * scale).astype(jnp.bfloat16)
        for d in range(1, R):
            wg_copy(d, r).start()

    @pl.when(sec == 0)
    def _():
        weight_along()

    spread = gath[...].reshape(R * nodes, width)

    def term(to):
        rows = pl.ds(pl.multiple_of(to * nodes, nodes), nodes)
        return jnp.dot(dense[rows, :], spread, preferred_element_type=jnp.float32)

    for d in range(1, C):
        part[d - 1] = term(lax.rem(c + d, C)).astype(jnp.bfloat16)
        col_copy(d).start()
    total = term(c)

    @pl.when(sec == 0)
    def _():
        weight_back()

    for d in range(1, C):
        col_copy(d).wait_recv()
        total = total + got[d - 1].astype(jnp.float32)
    feat[...] = total.astype(jnp.bfloat16)

    @pl.when(sec == 1)
    def _():
        hand_copy().start()
        weight_along()
        weight_back()
        hand_copy().wait_send()

    for d in range(1, R):
        wg_copy(d, lax.rem(r + R - d, R)).wait_recv()
    wsum[...] = summed[...].reshape(wsum.shape)
    for d in range(1, R):
        row_copy(d, r).wait_send()
        wx_copy(d).wait_send()
        wg_copy(d, r).wait_send()
    for d in range(1, C):
        col_copy(d).wait_send()
        wz_copy(d, c).wait_send()


def finish_kernel(wsum, feat, weight_grad, feature_grads):
    weight_grad[...] = wsum[...].astype(jnp.float32)
    feature_grads[...] = feat[...]


def fused(out_grad, pre_act, aggregated, weights, tiles, tile_index, live_count):
    R, C = lax.axis_size("row"), lax.axis_size("col")
    N = R * C
    nodes, width = out_grad.shape
    slot_total, block = tiles.shape[2:4]
    rows, cols = C * nodes, R * nodes
    row_blocks, col_blocks = rows // block, cols // block
    vmem = pl.BlockSpec(memory_space=pltpu.VMEM)
    smem = pl.BlockSpec(memory_space=pltpu.SMEM)
    bf16, f32, dma = jnp.bfloat16, jnp.float32, pltpu.SemaphoreType.DMA
    dense = pl.pallas_call(
        functools.partial(dense_kernel, col_blocks),
        out_shape=jax.ShapeDtypeStruct((rows, cols), bf16),
        in_specs=[smem, smem, pl.BlockSpec(memory_space=pl.ANY)],
        out_specs=vmem,
        scratch_shapes=[
            pltpu.VMEM((slot_total, block, block), bf16),
            pltpu.VMEM((row_blocks * col_blocks, block, block), f32),
            dma((CHUNKS,)),
        ],
        name="dense_tile",
    )(tile_index[0, 0].T, live_count, tiles[0, 0])
    share = width // R
    scale = 1.0 / math.sqrt(nodes * N)
    wsum, feat = pl.pallas_call(
        functools.partial(layers_kernel, R, C, scale),
        out_shape=(
            jax.ShapeDtypeStruct((width, width), bf16),
            jax.ShapeDtypeStruct((nodes, width), bf16),
        ),
        in_specs=[pl.BlockSpec(memory_space=pl.ANY)] * 5,
        out_specs=(vmem, vmem),
        scratch_shapes=[
            pltpu.VMEM((nodes, width), bf16),
            pltpu.VMEM((nodes, width), bf16),
            pltpu.VMEM((width, width), bf16),
            pltpu.VMEM((rows, cols), bf16),
            dma((5,)),
            pltpu.VMEM((nodes, width), bf16),
            pltpu.VMEM((R, nodes, width), bf16),
            pltpu.VMEM((C - 1, nodes, width), bf16),
            pltpu.VMEM((C - 1, nodes, width), bf16),
            pltpu.VMEM((R, share, width), bf16),
            pltpu.VMEM((R - 1, share, width), bf16),
            pltpu.VMEM((C, share, width), bf16),
            pltpu.VMEM((R, share, width), bf16),
            dma((R - 1,)), dma((R - 1,)), dma((C - 1,)), dma((C - 1,)), dma, dma,
            dma((R - 1,)), dma((R - 1,)), dma((C - 1,)), dma((C - 1,)), dma((R - 1,)), dma((R - 1,)),
        ],
        compiler_params=pltpu.CompilerParams(collective_id=0, has_side_effects=True),
        name="both_layers",
    )(out_grad, pre_act[0], aggregated[0], weights[0], dense)
    weight_grad, feature_grads = pl.pallas_call(
        finish_kernel,
        out_shape=(
            jax.ShapeDtypeStruct((width, width), f32),
            jax.ShapeDtypeStruct((nodes, width), bf16),
        ),
        in_specs=[vmem] * 2,
        out_specs=(vmem, vmem),
        name="finish",
    )(wsum, feat)
    return (weight_grad[None], feature_grads[None])


def from_behind(value, axis, steps):
    count = lax.axis_size(axis)
    leading, last = (max(0, -steps), min(count, count - steps))
    return lax.ppermute(value, axis, [(source, source + steps) for source in range(leading, last)])


def on_device(out_grad, pre_act, aggregated, weights, tiles, tile_index, live_count):
    nodes, width = out_grad.shape
    devices = lax.axis_size("row") * lax.axis_size("col")
    dense_blocks = devices * (nodes // tiles.shape[3]) ** 2
    if dense_blocks <= tiles.shape[2] and width % (16 * devices) == 0:
        return fused(out_grad, pre_act, aggregated, weights, tiles, tile_index, live_count)
    section_id = lax.axis_index("section")
    upper = section_id == 1
    pre_layer = pre_act[0]
    saved_agg = aggregated[0]
    weight_mat = weights[0]
    tile_blocks = tiles[0, 0]
    tile_slots = tile_index[0, 0]
    tile_count = live_count[0, 0]
    node_rows = out_grad.shape[0]
    width = out_grad.shape[1]
    slot_total = tile_blocks.shape[0]
    block = tile_blocks.shape[1]
    tile_rows = node_rows * lax.axis_size("col")
    row_blocks = tile_rows // block
    group = min(32, slot_total)
    groups = slot_total // group
    grouped_slots = tile_slots.reshape(groups, group, 2)
    all_targets = jnp.arange(row_blocks, dtype=jnp.int32)

    def spread(row_grad):
        return lax.all_gather(row_grad, "row", axis=0, tiled=True)

    def block_total(source, col_blocks):
        height = source.shape[1]
        grouped_blocks = source.reshape(groups, group, height, block)

        def group_term(total, blocks_here, slots_here, first_slot):
            picked = jnp.take(col_blocks, slots_here[:, 1], axis=0)
            products = jnp.einsum(
                "sij,sjf->sif", blocks_here, picked, preferred_element_type=jnp.float32
            )
            slot_ids = first_slot + jnp.arange(group, dtype=jnp.int32)
            live = slot_ids < tile_count
            select = ((slots_here[:, 0][None, :] == all_targets[:, None]) & live[None, :]).astype(
                jnp.float32
            )
            return total + jnp.einsum("bs,sif->bif", select, products)

        start_total = jnp.zeros((row_blocks, height, width), jnp.float32)

        def scan_step(total, group_id):
            blocks_here = lax.dynamic_index_in_dim(grouped_blocks, group_id, 0, False)
            slots_here = lax.dynamic_index_in_dim(grouped_slots, group_id, 0, False)
            return (group_term(total, blocks_here, slots_here, group_id * group), None)

        total, _ = lax.scan(scan_step, start_total, jnp.arange(groups, dtype=jnp.int32))
        return total.reshape(row_blocks * height, width)

    def reduce_col(source, gathered):
        col_blocks = gathered.reshape(-1, block, width)
        height = source.shape[1]
        return lax.psum_scatter(
            block_total(source, col_blocks), "col", scatter_dimension=0, tiled=True
        )

    def local_terms(incoming):
        masked = jnp.where(pre_layer > 0, incoming, jnp.zeros_like(incoming))
        weight_term = lax.dot_general(
            saved_agg, masked, (((0,), (0,)), ((), ())), preferred_element_type=jnp.float32
        )
        row_grad = lax.dot_general(
            masked, weight_mat, (((1,), (1,)), ((), ())), preferred_element_type=jnp.float32
        ).astype(jnp.bfloat16)
        return (weight_term, row_grad)

    def backward_step(incoming):
        weight_term, row_grad = local_terms(incoming)
        summed = reduce_col(tile_blocks, spread(row_grad))
        return (weight_term, summed.astype(jnp.bfloat16))

    first_input = jnp.where(upper, out_grad, jnp.zeros_like(out_grad))
    first_weight, first_grad = backward_step(first_input)
    received = from_behind(first_grad, "section", -1)
    second_weight, second_grad = backward_step(received)
    local_weight = jnp.where(upper, first_weight, second_weight)
    feature_block = jnp.where(upper, first_grad, second_grad)
    total_weight = lax.psum(local_weight, ("row", "col"))
    node_total = node_rows * lax.axis_size("row") * lax.axis_size("col")
    weight_grad = (total_weight * (1.0 / math.sqrt(node_total)))[None]
    return (weight_grad, feature_block[None])


def solution(mesh):
    placed = (
        P(("row", "col"), None),
        P("section", ("row", "col"), None),
        P("section", ("row", "col"), None),
        P("section", None, None),
        P("row", "col", None, None, None),
        P("row", "col", None, None),
        P("row", "col"),
    )
    return jax.shard_map(
        on_device,
        mesh=mesh,
        in_specs=placed,
        out_specs=(P("section", None, None), P("section", ("row", "col"), None)),
        check_vma=False,
    )
```

```python
import functools
import math

import jax
import jax.numpy as jnp
from jax import lax
from jax.experimental import pallas as pl
from jax.experimental.pallas import tpu as pltpu
from jax.sharding import PartitionSpec as P

MESH = pl.DeviceIdType.MESH
CHUNKS = 4


def dense_kernel(col_blocks, slots, count, tiles, dense, held, total, sems):
    slot_total, block = held.shape[:2]
    per = slot_total // CHUNKS

    def fetch(part):
        rows = pl.ds(part * per, per)
        return pltpu.make_async_copy(tiles.at[rows], held.at[rows], sems.at[part])

    for part in range(CHUNKS):
        fetch(part).start()
    total[...] = jnp.zeros_like(total)
    live = count[0, 0]

    def add(slot, carry):
        place = slots[0, slot] * col_blocks + slots[1, slot]
        total[place] += held[slot].astype(jnp.float32)
        return carry

    for part in range(CHUNKS):
        fetch(part).wait()
        lax.fori_loop(part * per, jnp.minimum(live, (part + 1) * per), add, 0)
    for place in range(total.shape[0]):
        r, c = divmod(place, col_blocks)
        dense[pl.ds(r * block, block), pl.ds(c * block, block)] = total[place].astype(jnp.bfloat16)


def layers_kernel(
    R, C, scale, out_grad, pre_act, aggregated, weights, dense_tile, wsum, feat,
    pre, agg, weight, dense, in_sems, inc, gath, part, got, wire, xgot, along, summed,
    row_send, row_recv, col_send, col_recv, hand_send, hand_recv,
    wx_send, wx_recv, wz_send, wz_recv, wg_send, wg_recv,
):
    sec, r, c = (lax.axis_index(a) for a in ("section", "row", "col"))
    nodes, width = inc.shape

    def row_peer(d):
        return (sec, lax.rem(r + d, R), c)

    def col_peer(d):
        return (sec, r, lax.rem(c + d, C))

    across = (1 - sec, r, c)
    barrier = pltpu.get_barrier_semaphore()
    peers = [row_peer(d) for d in range(1, R)] + [col_peer(d) for d in range(1, C)] + [across]
    for to in peers:
        pl.semaphore_signal(barrier, inc=1, device_id=to, device_id_type=MESH)

    load_inc = pltpu.make_async_copy(out_grad, inc, in_sems.at[0])
    load_pre = pltpu.make_async_copy(pre_act, pre, in_sems.at[1])
    load_weight = pltpu.make_async_copy(weights, weight, in_sems.at[2])
    load_agg = pltpu.make_async_copy(aggregated, agg, in_sems.at[3])
    load_dense = pltpu.make_async_copy(dense_tile, dense, in_sems.at[4])

    @pl.when(sec == 1)
    def _():
        load_inc.start()

    load_pre.start()
    load_weight.start()
    load_agg.start()
    load_dense.start()

    def copy(src, dst, send, recv, to):
        return pltpu.make_async_remote_copy(
            src_ref=src, dst_ref=dst, send_sem=send, recv_sem=recv, device_id=to, device_id_type=MESH
        )

    half = width // 2

    def row_copy(h, d, slot):
        k = h * (R - 1) + d - 1
        return copy(gath.at[h, slot], gath.at[h, slot], row_send.at[k], row_recv.at[k], row_peer(d))

    def col_copy(h, d):
        k = h * (C - 1) + d - 1
        return copy(part.at[k], got.at[k], col_send.at[k], col_recv.at[k], col_peer(d))

    def hand_copy():
        return copy(feat, inc, hand_send, hand_recv, across)

    def wx_copy(d):
        to = lax.rem(r + d, R)
        return copy(wire.at[to], xgot.at[d - 1], wx_send.at[d - 1], wx_recv.at[d - 1], row_peer(d))

    def wz_copy(d, slot):
        return copy(along.at[slot], along.at[slot], wz_send.at[d - 1], wz_recv.at[d - 1], col_peer(d))

    def wg_copy(d, slot):
        return copy(summed.at[slot], summed.at[slot], wg_send.at[d - 1], wg_recv.at[d - 1], row_peer(d))

    def own_rows():
        masked = jnp.where(pre[...] > 0, inc[...], jnp.zeros((nodes, width), jnp.bfloat16))
        inc[...] = masked
        rows = lax.dot_general(
            masked, weight[...], (((1,), (1,)), ((), ())), preferred_element_type=jnp.float32
        ).astype(jnp.bfloat16)
        gath[0, r] = rows[:, :half]
        gath[1, r] = rows[:, half:]

    load_pre.wait()
    load_weight.wait()

    @pl.when(sec == 1)
    def _():
        load_inc.wait()
        own_rows()

    pl.semaphore_wait(barrier, len(peers))

    @pl.when(sec == 0)
    def _():
        hand_copy().wait_recv()
        own_rows()

    for h in range(2):
        for d in range(1, R):
            row_copy(h, d, r).start()

    load_agg.wait()
    wire[...] = lax.dot_general(
        agg[...], inc[...], (((0,), (0,)), ((), ())), preferred_element_type=jnp.float32
    ).astype(jnp.bfloat16).reshape(wire.shape)
    for d in range(1, R):
        wx_copy(d).start()

    load_dense.wait()

    def weight_along():
        here = wire[r].astype(jnp.float32)
        for d in range(1, R):
            wx_copy(d).wait_recv()
            here = here + xgot[d - 1].astype(jnp.float32)
        along[c] = here.astype(jnp.bfloat16)
        for d in range(1, C):
            wz_copy(d, c).start()

    def weight_back():
        for d in range(1, C):
            wz_copy(d, lax.rem(c + C - d, C)).wait_recv()
        whole = along[0].astype(jnp.float32)
        for k in range(1, C):
            whole = whole + along[k].astype(jnp.float32)
        summed[r] = (whole * scale).astype(jnp.bfloat16)
        for d in range(1, R):
            wg_copy(d, r).start()

    totals = []
    for h in range(2):
        for d in range(1, R):
            row_copy(h, d, lax.rem(r + R - d, R)).wait_recv()
        if h == 1:
            @pl.when(sec == 0)
            def _():
                weight_along()
        spread = gath[h].reshape(R * nodes, half)

        def term(to):
            rows = pl.ds(pl.multiple_of(to * nodes, nodes), nodes)
            return jnp.dot(dense[rows, :], spread, preferred_element_type=jnp.float32)

        for d in range(1, C):
            part[h * (C - 1) + d - 1] = term(lax.rem(c + d, C)).astype(jnp.bfloat16)
            col_copy(h, d).start()
        totals.append(term(c))

    @pl.when(sec == 0)
    def _():
        weight_back()

    for h in range(2):
        total = totals[h]
        for d in range(1, C):
            col_copy(h, d).wait_recv()
            total = total + got[h * (C - 1) + d - 1].astype(jnp.float32)
        feat[:, h * half:(h + 1) * half] = total.astype(jnp.bfloat16)

    @pl.when(sec == 1)
    def _():
        hand_copy().start()
        weight_along()
        weight_back()
        hand_copy().wait_send()

    for d in range(1, R):
        wg_copy(d, lax.rem(r + R - d, R)).wait_recv()
    wsum[...] = summed[...].reshape(wsum.shape)
    for d in range(1, R):
        for h in range(2):
            row_copy(h, d, r).wait_send()
        wx_copy(d).wait_send()
        wg_copy(d, r).wait_send()
    for d in range(1, C):
        for h in range(2):
            col_copy(h, d).wait_send()
        wz_copy(d, c).wait_send()


def finish_kernel(wsum, feat, weight_grad, feature_grads):
    weight_grad[...] = wsum[...].astype(jnp.float32)
    feature_grads[...] = feat[...]


def fused(out_grad, pre_act, aggregated, weights, tiles, tile_index, live_count):
    R, C = lax.axis_size("row"), lax.axis_size("col")
    N = R * C
    nodes, width = out_grad.shape
    slot_total, block = tiles.shape[2:4]
    rows, cols = C * nodes, R * nodes
    row_blocks, col_blocks = rows // block, cols // block
    vmem = pl.BlockSpec(memory_space=pltpu.VMEM)
    smem = pl.BlockSpec(memory_space=pltpu.SMEM)
    bf16, f32, dma = jnp.bfloat16, jnp.float32, pltpu.SemaphoreType.DMA
    dense = pl.pallas_call(
        functools.partial(dense_kernel, col_blocks),
        out_shape=jax.ShapeDtypeStruct((rows, cols), bf16),
        in_specs=[smem, smem, pl.BlockSpec(memory_space=pl.ANY)],
        out_specs=vmem,
        scratch_shapes=[
            pltpu.VMEM((slot_total, block, block), bf16),
            pltpu.VMEM((row_blocks * col_blocks, block, block), f32),
            dma((CHUNKS,)),
        ],
        name="dense_tile",
    )(tile_index[0, 0].T, live_count, tiles[0, 0])
    share = width // R
    scale = 1.0 / math.sqrt(nodes * N)
    wsum, feat = pl.pallas_call(
        functools.partial(layers_kernel, R, C, scale),
        out_shape=(
            jax.ShapeDtypeStruct((width, width), bf16),
            jax.ShapeDtypeStruct((nodes, width), bf16),
        ),
        in_specs=[pl.BlockSpec(memory_space=pl.ANY)] * 5,
        out_specs=(vmem, vmem),
        scratch_shapes=[
            pltpu.VMEM((nodes, width), bf16),
            pltpu.VMEM((nodes, width), bf16),
            pltpu.VMEM((width, width), bf16),
            pltpu.VMEM((rows, cols), bf16),
            dma((5,)),
            pltpu.VMEM((nodes, width), bf16),
            pltpu.VMEM((2, R, nodes, width // 2), bf16),
            pltpu.VMEM((2 * (C - 1), nodes, width // 2), bf16),
            pltpu.VMEM((2 * (C - 1), nodes, width // 2), bf16),
            pltpu.VMEM((R, share, width), bf16),
            pltpu.VMEM((R - 1, share, width), bf16),
            pltpu.VMEM((C, share, width), bf16),
            pltpu.VMEM((R, share, width), bf16),
            dma((2 * (R - 1),)), dma((2 * (R - 1),)), dma((2 * (C - 1),)), dma((2 * (C - 1),)), dma, dma,
            dma((R - 1,)), dma((R - 1,)), dma((C - 1,)), dma((C - 1,)), dma((R - 1,)), dma((R - 1,)),
        ],
        compiler_params=pltpu.CompilerParams(collective_id=0, has_side_effects=True),
        name="both_layers",
    )(out_grad, pre_act[0], aggregated[0], weights[0], dense)
    weight_grad, feature_grads = pl.pallas_call(
        finish_kernel,
        out_shape=(
            jax.ShapeDtypeStruct((width, width), f32),
            jax.ShapeDtypeStruct((nodes, width), bf16),
        ),
        in_specs=[vmem] * 2,
        out_specs=(vmem, vmem),
        name="finish",
    )(wsum, feat)
    return (weight_grad[None], feature_grads[None])


def from_behind(value, axis, steps):
    count = lax.axis_size(axis)
    leading, last = (max(0, -steps), min(count, count - steps))
    return lax.ppermute(value, axis, [(source, source + steps) for source in range(leading, last)])


def on_device(out_grad, pre_act, aggregated, weights, tiles, tile_index, live_count):
    nodes, width = out_grad.shape
    devices = lax.axis_size("row") * lax.axis_size("col")
    dense_blocks = devices * (nodes // tiles.shape[3]) ** 2
    if dense_blocks <= tiles.shape[2] and width % (16 * devices) == 0:
        return fused(out_grad, pre_act, aggregated, weights, tiles, tile_index, live_count)
    section_id = lax.axis_index("section")
    upper = section_id == 1
    pre_layer = pre_act[0]
    saved_agg = aggregated[0]
    weight_mat = weights[0]
    tile_blocks = tiles[0, 0]
    tile_slots = tile_index[0, 0]
    tile_count = live_count[0, 0]
    node_rows = out_grad.shape[0]
    width = out_grad.shape[1]
    slot_total = tile_blocks.shape[0]
    block = tile_blocks.shape[1]
    tile_rows = node_rows * lax.axis_size("col")
    row_blocks = tile_rows // block
    group = min(32, slot_total)
    groups = slot_total // group
    grouped_slots = tile_slots.reshape(groups, group, 2)
    all_targets = jnp.arange(row_blocks, dtype=jnp.int32)

    def spread(row_grad):
        return lax.all_gather(row_grad, "row", axis=0, tiled=True)

    def block_total(source, col_blocks):
        height = source.shape[1]
        grouped_blocks = source.reshape(groups, group, height, block)

        def group_term(total, blocks_here, slots_here, first_slot):
            picked = jnp.take(col_blocks, slots_here[:, 1], axis=0)
            products = jnp.einsum(
                "sij,sjf->sif", blocks_here, picked, preferred_element_type=jnp.float32
            )
            slot_ids = first_slot + jnp.arange(group, dtype=jnp.int32)
            live = slot_ids < tile_count
            select = ((slots_here[:, 0][None, :] == all_targets[:, None]) & live[None, :]).astype(
                jnp.float32
            )
            return total + jnp.einsum("bs,sif->bif", select, products)

        start_total = jnp.zeros((row_blocks, height, width), jnp.float32)

        def scan_step(total, group_id):
            blocks_here = lax.dynamic_index_in_dim(grouped_blocks, group_id, 0, False)
            slots_here = lax.dynamic_index_in_dim(grouped_slots, group_id, 0, False)
            return (group_term(total, blocks_here, slots_here, group_id * group), None)

        total, _ = lax.scan(scan_step, start_total, jnp.arange(groups, dtype=jnp.int32))
        return total.reshape(row_blocks * height, width)

    def reduce_col(source, gathered):
        col_blocks = gathered.reshape(-1, block, width)
        height = source.shape[1]
        return lax.psum_scatter(
            block_total(source, col_blocks), "col", scatter_dimension=0, tiled=True
        )

    def local_terms(incoming):
        masked = jnp.where(pre_layer > 0, incoming, jnp.zeros_like(incoming))
        weight_term = lax.dot_general(
            saved_agg, masked, (((0,), (0,)), ((), ())), preferred_element_type=jnp.float32
        )
        row_grad = lax.dot_general(
            masked, weight_mat, (((1,), (1,)), ((), ())), preferred_element_type=jnp.float32
        ).astype(jnp.bfloat16)
        return (weight_term, row_grad)

    def backward_step(incoming):
        weight_term, row_grad = local_terms(incoming)
        summed = reduce_col(tile_blocks, spread(row_grad))
        return (weight_term, summed.astype(jnp.bfloat16))

    first_input = jnp.where(upper, out_grad, jnp.zeros_like(out_grad))
    first_weight, first_grad = backward_step(first_input)
    received = from_behind(first_grad, "section", -1)
    second_weight, second_grad = backward_step(received)
    local_weight = jnp.where(upper, first_weight, second_weight)
    feature_block = jnp.where(upper, first_grad, second_grad)
    total_weight = lax.psum(local_weight, ("row", "col"))
    node_total = node_rows * lax.axis_size("row") * lax.axis_size("col")
    weight_grad = (total_weight * (1.0 / math.sqrt(node_total)))[None]
    return (weight_grad, feature_block[None])


def solution(mesh):
    placed = (
        P(("row", "col"), None),
        P("section", ("row", "col"), None),
        P("section", ("row", "col"), None),
        P("section", None, None),
        P("row", "col", None, None, None),
        P("row", "col", None, None),
        P("row", "col"),
    )
    return jax.shard_map(
        on_device,
        mesh=mesh,
        in_specs=placed,
        out_specs=(P("section", None, None), P("section", ("row", "col"), None)),
        check_vma=False,
    )
```
